256 devices in a mesh: seq: 64 (over y, z, core), head: 4 (over x).
Axes of the slice: x: 4, y: 4, z: 8, core: 2. Of those that a mesh axis runs over, the one named last changes fastest.
Arguments:
- queries: bfloat16 [32768, 2048], P('seq', 'head'), may hold values from -5 to 5
- keys: bfloat16 [32768, 2048], P('seq', 'head'), may hold values from -5 to 5
- values: bfloat16 [32768, 2048], P('seq', 'head'), may hold values from -5 to 5
- out_weight: bfloat16 [2048, 2048], P('head'), may hold values from -0.125 to 0.125
- out_grad: bfloat16 [32768, 2048], P('seq'), may hold values from -5 to 5
- global_pos: int32 [256], replicated, may hold values from 0 to 511, as said below
- block_mask: int32 [256, 4], P('seq'), may hold values 0 or 1
Outputs:
- layer_out: bfloat16 [32768, 2048], P('seq', 'head')
- grad_queries: bfloat16 [32768, 2048], P('seq', 'head')
- grad_keys: bfloat16 [32768, 2048], P('seq', 'head')
- grad_values: bfloat16 [32768, 2048], P('seq', 'head')
The draws below stay inside these ranges and needn't reach their ends.
Inputs may be any that keep to these rules, and one draw needn't show every extreme that they name: `global_pos`: 256 distinct positions among the first 512 tokens.
All inputs are finite; a program needn't handle non-finite values. No bound on the sum of `block_mask` on one device may be relied on, other than what follows from the above.
Results may differ from the reference program's by a relative error of at most 0.012.
Values may be sent and summed in bfloat16 or wider, within the bound.
A program may use at most 192 MiB of HBM per device.

```python
import math
import jax
import jax.numpy as jnp
from jax import lax

HEADS = 16
HEAD_DIM = 128
D = 2048
BLOCK = 128
WBLK = 4
GLOBALS = 256
TOK_DEV = 512
TOKENS = 32768
NBLK = 256


def draw_queries(key, part):
    own_key = jax.random.fold_in(key, 1)
    return jnp.clip(jax.random.normal(own_key, (TOKENS, D), jnp.float32), -4.0, 4.0).astype(jnp.bfloat16)


def draw_keys(key, part):
    own_key = jax.random.fold_in(key, 2)
    return jnp.clip(jax.random.normal(own_key, (TOKENS, D), jnp.float32), -4.0, 4.0).astype(jnp.bfloat16)


def draw_global_pos(key, part):
    inner = jax.random.permutation(key, TOK_DEV - 2)[:GLOBALS - 2].astype(jnp.int32) + 1
    both = jnp.concatenate([jnp.array([0, TOK_DEV - 1], jnp.int32), inner])
    order = jax.random.permutation(jax.random.fold_in(key, 3), GLOBALS)
    return both[order]


def with_ends(entries, rng, smallest, top_value):
    longest = entries.shape.index(max(entries.shape))
    spots = []
    for shift in (0, 1):
        where = [jax.random.randint(jax.random.fold_in(rng, axis), (), 0, length) for axis, length in enumerate(entries.shape)]
        where[longest] = (where[longest] + shift) % entries.shape[longest]
        spots.append(tuple(where))
    return entries.at[spots[0]].set(smallest).at[spots[1]].set(top_value)


def shard_levels(key, dims, split, low, high):
    loudness, own = 1.0, jax.random.fold_in(key, 6)
    for axis_at, parts in split:
        steps = jnp.exp(jax.random.uniform(jax.random.fold_in(own, axis_at), (parts,), jnp.float32, low / len(split), high / len(split)))
        loudness = loudness * jnp.repeat(steps, dims[axis_at] // parts).reshape([-1 if axis == axis_at else 1 for axis in range(len(dims))])
    return loudness


def gaussian(stream_key, shape, spread, reach, split=(), kind=jnp.bfloat16):
    drawn = jax.random.normal(stream_key, shape, jnp.float32) * spread
    if len(split) > 0:
        drawn = shard_levels(stream_key, shape, split, -0.22, 0.18) * drawn
    return jnp.clip(drawn, min=-reach, max=reach).astype(kind)


def setup_inputs(seed: int = 0) -> dict:
    seeds = jax.random.split(jax.random.key(seed), 8)
    queries = draw_queries(jax.random.fold_in(seeds[7], 71), 0)
    keys = draw_keys(jax.random.fold_in(seeds[7], 71), 0)
    values = gaussian(seeds[2], (TOKENS, D), 1.0, 5.0, ((0, 64), (1, 4)))
    out_weight = gaussian(seeds[3], (D, D), D ** -0.5, 0.125, ((0, 4),))
    out_grad = gaussian(seeds[4], (TOKENS, D), 1.0, 5.0, ((0, 64),))
    global_pos = draw_global_pos(jax.random.fold_in(seeds[7], 71), 0)
    block_mask = with_ends((jax.random.randint(seeds[6], (NBLK, WBLK), 0, 4) < 3).astype(jnp.int32), jax.random.fold_in(seeds[6], 1), 0, 1)
    return {"queries": queries, "keys": keys, "values": values, "out_weight": out_weight, "out_grad": out_grad, "global_pos": global_pos, "block_mask": block_mask}


def window_view(matrix):
    lead_rows = (WBLK - 1) * BLOCK
    padded = jnp.concatenate([jnp.zeros((lead_rows,) + matrix.shape[1:], matrix.dtype), matrix], axis=0)
    blocks = padded.reshape((NBLK + WBLK - 1, BLOCK) + matrix.shape[1:])
    return jnp.stack([blocks[WBLK - 1 - offset:WBLK - 1 - offset + NBLK] for offset in range(WBLK)], axis=1)

def window_fold(window_terms):
    summed = jnp.zeros((NBLK + WBLK - 1,) + window_terms.shape[2:], jnp.float32)
    for offset in range(WBLK):
        summed = summed.at[WBLK - 1 - offset:WBLK - 1 - offset + NBLK].add(window_terms[:, offset])
    return summed[WBLK - 1:].reshape((TOKENS,) + window_terms.shape[3:])

def rounded(values_f32):
    return lax.optimization_barrier(values_f32.astype(jnp.bfloat16)).astype(jnp.float32)

def reference(queries, keys, values, out_weight, out_grad, global_pos, block_mask):
    exact_prec = lax.Precision.HIGHEST
    score_scale = 1.0 / math.sqrt(HEAD_DIM)
    is_global = jnp.zeros((TOKENS,), jnp.int32).at[global_pos].set(1) > 0
    d_attn = jnp.dot(out_grad, out_weight.T, preferred_element_type=jnp.float32).astype(jnp.bfloat16)
    block_idx = jnp.arange(NBLK)[:, None, None, None]
    rel_block = jnp.arange(WBLK)[None, None, :, None]
    query_in = jnp.arange(BLOCK)[None, :, None, None]
    key_in = jnp.arange(BLOCK)[None, None, None, :]
    block_ok = block_mask[:, None, :, None] == 1
    key_global = window_view(is_global.astype(jnp.int32))[:, None, :, :] > 0
    pair_ok = (block_idx - rel_block >= 0) & block_ok & ((rel_block > 0) | (key_in <= query_in)) & jnp.logical_not(key_global)

    def one_head(operands):
        query_head, key_head, value_head, dattn_head = operands
        query_f = query_head.astype(jnp.float32)
        key_f = key_head.astype(jnp.float32)
        value_f = value_head.astype(jnp.float32)
        dattn_f = dattn_head.astype(jnp.float32)
        query_blk = query_f.reshape(NBLK, BLOCK, HEAD_DIM)
        key_win = window_view(key_f)
        value_win = window_view(value_f)
        key_glob = key_f[global_pos]
        value_glob = value_f[global_pos]
        win_scores = jnp.einsum('bid,brjd->birj', query_blk, key_win, precision=exact_prec) * score_scale
        win_scores = jnp.where(pair_ok, win_scores, -jnp.inf)
        glob_scores = jnp.einsum('bid,gd->big', query_blk, key_glob, precision=exact_prec) * score_scale
        row_peak = jnp.maximum(lax.optimization_barrier(jnp.max(win_scores, axis=(2, 3))), lax.optimization_barrier(jnp.max(glob_scores, axis=2)))
        row_mass = lax.optimization_barrier(jnp.sum(jnp.exp(win_scores - row_peak[:, :, None, None]), axis=(2, 3))) + lax.optimization_barrier(jnp.sum(jnp.exp(glob_scores - row_peak[:, :, None]), axis=2))
        row_lse = row_peak + jnp.log(row_mass)
        win_prob = jnp.exp(win_scores - row_lse[:, :, None, None])
        glob_prob = jnp.exp(glob_scores - row_lse[:, :, None])
        win_weight = rounded(win_prob)
        glob_weight = rounded(glob_prob)
        attn_win = jnp.einsum('birj,brjd->bid', win_weight, value_win, precision=exact_prec) + jnp.einsum('big,gd->bid', glob_weight, value_glob, precision=exact_prec)
        attn_win = attn_win.reshape(TOKENS, HEAD_DIM)
        query_rows = query_f[global_pos]
        row_scores = jnp.dot(query_rows, key_f.T, precision=exact_prec) * score_scale
        rows_peak = lax.optimization_barrier(jnp.max(row_scores, axis=1))
        rows_lse = rows_peak + jnp.log(lax.optimization_barrier(jnp.sum(jnp.exp(row_scores - rows_peak[:, None]), axis=1)))
        row_prob = jnp.exp(row_scores - rows_lse[:, None])
        attn_rows = jnp.dot(row_prob, value_f, precision=exact_prec)
        attn_bf = attn_win.at[global_pos].set(attn_rows).astype(jnp.bfloat16)
        attn_f = lax.optimization_barrier(attn_bf).astype(jnp.float32)
        dattn_win = jnp.where(is_global[:, None], 0.0, dattn_f)
        delta_win = lax.optimization_barrier(jnp.sum(dattn_win * attn_f, axis=1)).reshape(NBLK, BLOCK)
        dattn_blk = dattn_win.reshape(NBLK, BLOCK, HEAD_DIM)
        win_dprob = jnp.einsum('bid,brjd->birj', dattn_blk, value_win, precision=exact_prec)
        glob_dprob = jnp.einsum('bid,gd->big', dattn_blk, value_glob, precision=exact_prec)
        win_dscore = rounded(win_prob * (win_dprob - delta_win[:, :, None, None]))
        glob_dscore = rounded(glob_prob * (glob_dprob - delta_win[:, :, None]))
        dq_win = jnp.einsum('birj,brjd->bid', win_dscore, key_win, precision=exact_prec) + jnp.einsum('big,gd->bid', glob_dscore, key_glob, precision=exact_prec)
        dq_win = dq_win.reshape(TOKENS, HEAD_DIM)
        dk_win = window_fold(jnp.einsum('birj,bid->brjd', win_dscore, query_blk, precision=exact_prec))
        dk_win = dk_win.at[global_pos].add(jnp.einsum('big,bid->gd', glob_dscore, query_blk, precision=exact_prec))
        dv_win = window_fold(jnp.einsum('birj,bid->brjd', win_weight, dattn_blk, precision=exact_prec))
        dv_win = dv_win.at[global_pos].add(jnp.einsum('big,bid->gd', glob_weight, dattn_blk, precision=exact_prec))
        dattn_rows = dattn_f[global_pos]
        delta_rows = lax.optimization_barrier(jnp.sum(dattn_rows * attn_f[global_pos], axis=1))
        row_dprob = jnp.dot(dattn_rows, value_f.T, precision=exact_prec)
        row_dscore = rounded(row_prob * (row_dprob - delta_rows[:, None]))
        row_weight = rounded(row_prob)
        grad_q = dq_win.at[global_pos].add(jnp.dot(row_dscore, key_f, precision=exact_prec)) * score_scale
        grad_k = (dk_win + jnp.dot(row_dscore.T, query_rows, precision=exact_prec)) * score_scale
        grad_v = dv_win + jnp.dot(row_weight.T, dattn_rows, precision=exact_prec)
        return (attn_bf, grad_q.astype(jnp.bfloat16), grad_k.astype(jnp.bfloat16), grad_v.astype(jnp.bfloat16))

    def split_heads(matrix):
        return matrix.reshape(TOKENS, HEADS, HEAD_DIM).transpose(1, 0, 2)

    def merge_heads(stacked):
        return stacked.transpose(1, 0, 2).reshape(TOKENS, D)
    attn_all, grad_q_all, grad_k_all, grad_v_all = lax.map(one_head, (split_heads(queries), split_heads(keys), split_heads(values), split_heads(d_attn)))
    layer_out = jnp.dot(merge_heads(attn_all), out_weight, preferred_element_type=jnp.float32).astype(jnp.bfloat16)
    return (layer_out, merge_heads(grad_q_all), merge_heads(grad_k_all), merge_heads(grad_v_all))
```

```python
import math

import jax
import jax.numpy as jnp
from jax import lax
from jax.experimental import pallas as pl
from jax.experimental.pallas import tpu as pltpu
from jax.sharding import PartitionSpec as P

HD = 128
BLK = 128
WBLK = 4
GLB = 256
TOK = 512
COLS = 512
LH = 4
NB = 4
RIM = 384
D = 2048
NY = 4
NZ = 8
NS = 64
NX = 4
NCH = 16
SCALE = 1.0 / math.sqrt(HD)
NEG = -1e30
F32 = jnp.float32
BF = jnp.bfloat16
MESH = pl.DeviceIdType.MESH


def mm(a, b):
    return lax.dot_general(a, b, (((1,), (0,)), ((), ())), preferred_element_type=F32)


def mm_t(a, b):
    return lax.dot_general(a, b, (((1,), (1,)), ((), ())), preferred_element_type=F32)


def flag(cond):
    return jnp.where(cond, 1, 0).astype(jnp.int32)


def kernel(
    q_hbm, k_hbm, v_hbm, w_hbm, og_hbm, gpos, bmask,
    lo_out, gq_out, gk_out, gv_out,
    q_s, kc, vc, w_s, og_s, da_s, oh_s, gbuf, bias,
    ew, dpw, mw, lw, cw, uw, pg_s, attn_s,
    lp, lr, dkc, dvc, dqa, dkg, dvg, hbs, hbr,
    st1, st2, st3, srt, dpt,
    rb, sib, comb, rs, sl, ogat, rt,
    ld_sem, bs_send, bs_recv, halo_send, halo_recv, hb_send_sem, hb_recv_sem,
    lx_send, lx_recv, s1_send, s1_recv, s2_send, s2_recv, s3_send, s3_recv,
    sib_send, sib_recv, rs_send, rs_recv, og_send, og_recv,
):
    s = lax.axis_index("seq")
    x = lax.axis_index("head")
    core = s % 2
    chip = s // 2
    z = chip % NZ
    y = chip // NZ
    owner = s == 0
    mate = s + 1 - 2 * core

    def seq_of(yy, zz, cc):
        return (yy * NZ + zz) * 2 + cc

    def remote(src, dst, ssem, rsem, to_seq):
        return pltpu.make_async_remote_copy(
            src_ref=src, dst_ref=dst, send_sem=ssem, recv_sem=rsem,
            device_id={"seq": to_seq}, device_id_type=MESH)

    loads = [
        pltpu.make_async_copy(k_hbm, kc.at[pl.ds(RIM, TOK)], ld_sem.at[0]),
        pltpu.make_async_copy(v_hbm, vc.at[pl.ds(RIM, TOK)], ld_sem.at[1]),
        pltpu.make_async_copy(q_hbm, q_s, ld_sem.at[2]),
        pltpu.make_async_copy(og_hbm, og_s, ld_sem.at[3]),
        pltpu.make_async_copy(w_hbm, w_s, ld_sem.at[4]),
    ]
    for copy in loads:
        copy.start()
    for copy in loads[:3]:
        copy.wait()

    nxt = jnp.minimum(s + 1, NS - 1)
    prv = jnp.maximum(s - 1, 0)
    halo = [
        remote(buf.at[pl.ds(RIM + BLK, RIM)], buf.at[pl.ds(0, RIM)], halo_send.at[i], halo_recv.at[i], nxt)
        for i, buf in enumerate((kc, vc))
    ]

    @pl.when(s < NS - 1)
    def _():
        for copy in halo:
            copy.start()

    @pl.when(owner)
    def _():
        kc[pl.ds(0, RIM), :] = jnp.zeros((RIM, COLS), BF)
        vc[pl.ds(0, RIM), :] = jnp.zeros((RIM, COLS), BF)

    hits = jnp.where(
        lax.broadcasted_iota(jnp.int32, (TOK, GLB), 0) == gpos[...], 1.0, 0.0).astype(F32)
    is_row = jnp.max(hits.T, axis=0, keepdims=True)
    own_f = jnp.where(owner, 1.0, 0.0).astype(F32)
    one_f = jnp.where(s == 1, 1.0, 0.0).astype(F32)
    oh_s[...] = (hits * own_f).astype(BF)

    def tree(a, na, b, nb):
        ap = flag(b == 0) * flag(a < na // 2)
        am = flag(b == 0) * (flag(a == 0) + flag(a > na // 2 + 1)) + flag(b != 0) * flag(a == 1)
        bp = flag(a != 0) * flag(b < nb // 2)
        bm = flag(a != 0) * (flag(b == 0) + flag(b > nb // 2 + 1))
        return ap, am, bp, bm

    zp0, zm0, yp0, ym0 = tree(z, NZ, y, NY)
    yp1, ym1, zp1, zm1 = tree(y, NY, z, NZ)
    dirs = (
        (zp0, zp1, seq_of(y, (z + 1) % NZ, 0)),
        (zm0, zm1, seq_of(y, (z + NZ - 1) % NZ, 0)),
        (yp0, yp1, seq_of((y + 1) % NY, z, 0)),
        (ym0, ym1, seq_of((y + NY - 1) % NY, z, 0)),
    )

    def chunk(c):
        start = pl.multiple_of(((c // 2) % 2) * 128, 128)
        return gbuf.at[(c // 4) * 2 + c % 2, pl.ds(start, 128), :]

    def chunk_sends(c, act):
        half = c % 2
        for d, (c0, c1, dev) in enumerate(dirs):
            @pl.when((c0 * (1 - half) + c1 * half) * (1 - core) > 0)
            def _():
                act(remote(chunk(c), chunk(c), bs_send.at[c, d], bs_recv.at[c], dev))

        @pl.when(core == 0)
        def _():
            act(remote(chunk(c), chunk(c), bs_send.at[c, 4], bs_recv.at[c], mate))

    def gather(slot, src):
        got = mm(oh_s[...].astype(F32).T.astype(BF), src).astype(BF)
        gbuf[slot * 2, :, :] = got[:, :256]
        gbuf[slot * 2 + 1, :, :] = got[:, 256:]

    def send_chunks(first):
        @pl.loop(first, first + 8)
        def _(c):
            chunk_sends(c, lambda copy: copy.start())

    @pl.when(owner)
    def _():
        gather(0, q_s[...])
        gather(1, kc[pl.ds(RIM, TOK), :])
        send_chunks(0)

    for copy in loads[3:]:
        copy.wait()

    @pl.loop(0, NB)
    def _(b):
        rows = pl.ds(pl.multiple_of(b * BLK, BLK), BLK)
        da_s[rows, :] = mm_t(og_s[rows, :], w_s[...]).astype(BF)

    @pl.when(owner)
    def _():
        gather(2, da_s[...])
        gather(3, vc[pl.ds(RIM, TOK), :])
        send_chunks(8)
        is_col = jnp.max(oh_s[...].astype(F32), axis=1, keepdims=True)
        da_s[...] = jnp.where(is_col > 0, 0.0, da_s[...].astype(F32)).astype(BF)

    f_rim = is_row[:, 128:512] * one_f
    f_loc = is_row * own_f
    ii = lax.broadcasted_iota(jnp.int32, (BLK, BLK), 0)
    jj = lax.broadcasted_iota(jnp.int32, (BLK, BLK), 1)
    causal = jnp.where(jj <= ii, 0.0, NEG)
    for b in range(NB):
        for part in range(WBLK):
            r = WBLK - 1 - part
            ok = flag(bmask[b, r] == 1) * flag(s * NB + b - r >= 0)
            base = jnp.where(ok == 1, 0.0, NEG).astype(F32)
            at = b + part
            tok = f_rim[:, at * 128:(at + 1) * 128] if at < 3 else f_loc[:, (at - 3) * 128:(at - 2) * 128]
            tile = jnp.broadcast_to(tok * NEG + base, (BLK, BLK))
            if r == 0:
                tile = tile + causal
            bias[b, :, part * 128:(part + 1) * 128] = tile

    dkc[...] = jnp.zeros(dkc.shape, F32)
    dvc[...] = jnp.zeros(dvc.shape, F32)
    dkg[...] = jnp.zeros(dkg.shape, F32)
    dvg[...] = jnp.zeros(dvg.shape, F32)

    def spans(b, h):
        row0 = pl.multiple_of(b * BLK, BLK)
        return pl.ds(row0, BLK), pl.ds(row0, WBLK * BLK), pl.ds(pl.multiple_of(h * HD, HD), HD)

    def window_unit(u):
        b = NB - 1 - u // LH
        h = u % LH
        rows, win, cols = spans(b, h)
        sc = mm_t(q_s[rows, cols], kc[win, cols]) * SCALE + bias[b]
        top = jnp.max(sc, axis=1, keepdims=True)
        ex = jnp.exp(sc - top)
        i = b * LH + h
        ew[i] = ex
        mw[i] = top
        lw[i] = jnp.sum(ex, axis=1, keepdims=True)
        uw[rows, cols] = mm(ex.astype(BF), vc[win, cols])
        dpw[i] = mm_t(da_s[rows, cols], vc[win, cols])

    dz = jnp.minimum(z, NZ - z)
    dy = jnp.minimum(y, NY - y)
    depth = dz + dy
    leaf = flag(depth > 5) + core
    late_units = jnp.where(leaf > 0, 0, jnp.maximum(16 - 4 * depth, 0))
    late_relay = jnp.where(leaf > 0, 16, jnp.where(depth == 5, 4, 0))

    @pl.loop(0, 32)
    def _(t):
        u = jnp.where(t < 4, t, t - late_units)

        @pl.when((t >= 4) & (u == 4) & (s > 0))
        def _():
            for copy in halo:
                copy.wait_recv()

        @pl.when((t < 4) | ((u >= 4) & (u < 16)))
        def _():
            window_unit(u)

        c = t - late_relay

        @pl.when((c >= 0) & (c < NCH) & (s > 0))
        def _():
            remote(chunk(c), chunk(c), bs_send.at[c, 0], bs_recv.at[c], mate).wait_recv()
            chunk_sends(c, lambda copy: copy.start())

    def glob(slot, h):
        return gbuf[slot * 2 + h // 2, :, pl.ds(pl.multiple_of((h % 2) * HD, HD), HD)]

    @pl.loop(0, LH)
    def _(h):
        cols = pl.ds(pl.multiple_of(h * HD, HD), HD)
        loc = pl.ds(RIM, TOK)
        sc = mm_t(kc[loc, cols], glob(0, h)) * SCALE
        dp = mm_t(vc[loc, cols], glob(2, h))
        top = jnp.max(sc, axis=0, keepdims=True)
        ex = jnp.exp(sc - top)
        srt[h] = sc
        dpt[h] = dp
        st1[core, pl.ds(h, 1), :] = top
        st1[core, pl.ds(h + 4, 1), :] = jnp.sum(ex, axis=0, keepdims=True)
        st1[core, pl.ds(h + 8, 1), :] = jnp.sum(ex * dp, axis=0, keepdims=True)

    st1_copy = remote(st1.at[core], st1.at[core], s1_send.at[0], s1_recv.at[0], mate)
    st1_copy.start()

    def merge(ref, n):
        top = ref[0, 0:4, :]
        for i in range(1, n):
            top = jnp.maximum(top, ref[i, 0:4, :])
        tot = jnp.zeros((4, GLB), F32)
        dot = jnp.zeros((4, GLB), F32)
        for i in range(n):
            f = jnp.exp(ref[i, 0:4, :] - top)
            tot = tot + f * ref[i, 4:8, :]
            dot = dot + f * ref[i, 8:12, :]
        return top, tot, dot

    def put(ref, i, stats):
        for j, value in enumerate(stats):
            ref[i, j * 4:(j + 1) * 4, :] = value

    def lx_copies(b):
        rows = pl.ds(b * BLK, BLK)
        return [
            pltpu.make_async_remote_copy(
                src_ref=lp.at[(x + d) % NX, rows], dst_ref=lr.at[d - 1, rows],
                send_sem=lx_send.at[b, d - 1], recv_sem=lx_recv.at[b, d - 1],
                device_id={"head": (x + d) % NX}, device_id_type=MESH)
            for d in range(1, NX)
        ]

    def project(b):
        rows = pl.ds(b * BLK, BLK)
        for n in range(NX):
            lp[n, rows, :] = mm(attn_s[rows, :], w_s[:, n * COLS:(n + 1) * COLS]).astype(BF)
        for copy in lx_copies(b):
            copy.start()

    def forward(b):
        @pl.loop(0, LH)
        def _(h):
            rows, _, cols = spans(b, h)
            i = b * LH + h
            sg = mm_t(q_s[rows, cols], glob(1, h)) * SCALE
            top = jnp.maximum(mw[i], jnp.max(sg, axis=1, keepdims=True))
            eg = jnp.exp(sg - top)
            fac = jnp.exp(mw[i] - top)
            inv = 1.0 / (lw[i] * fac + jnp.sum(eg, axis=1, keepdims=True))
            out = (uw[rows, cols] * fac + mm(eg.astype(BF), glob(3, h))) * inv
            attn_s[rows, cols] = out.astype(BF)
            cw[i] = fac * inv
            pg_s[i] = eg * inv

        @pl.when(s > 0)
        def _():
            project(b)

    forward(0)
    st1_copy.wait()
    put(st2, y, merge(st1, 2))
    st2_copies = [
        remote(st2.at[y], st2.at[y], s2_send.at[d - 1], s2_recv.at[d - 1], seq_of((y + d) % NY, z, core))
        for d in range(1, NY)
    ]
    for copy in st2_copies:
        copy.start()
    forward(1)
    for d in range(1, NY):
        src = (y + NY - d) % NY
        remote(st2.at[src], st2.at[src], s2_send.at[d - 1], s2_recv.at[d - 1], mate).wait_recv()
    put(st3, z, merge(st2, NY))
    st3_copies = [
        remote(st3.at[z], st3.at[z], s3_send.at[d - 1], s3_recv.at[d - 1], seq_of(y, (z + d) % NZ, core))
        for d in range(1, NZ)
    ]
    for copy in st3_copies:
        copy.start()
    forward(2)
    forward(3)

    @pl.loop(0, NB * LH)
    def _(i):
        b = i // LH
        h = i % LH
        rows, _, cols = spans(b, h)
        da = da_s[rows, cols]
        delta = jnp.sum(da.astype(F32) * attn_s[rows, cols].astype(F32), axis=1, keepdims=True)
        pg = pg_s[i]
        ds = pg * (mm_t(da, glob(3, h)) - delta)
        dqa[rows, cols] = mm(ds.astype(BF), glob(1, h))
        dkg[:, cols] += mm(ds.T.astype(BF), q_s[rows, cols])
        dvg[:, cols] += mm(pg.T.astype(BF), da)

    def sib_copy(t):
        return remote(rb.at[t * 2 + 1 - core], sib.at[t], sib_send.at[t], sib_recv.at[t], mate)

    for t, part in ((2, dkg), (3, dvg)):
        for half in range(2):
            rb[t * 2 + half] = part[:, half * 256:(half + 1) * 256].astype(BF)
        sib_copy(t).start()

    for d in range(1, NZ):
        src = (z + NZ - d) % NZ
        remote(st3.at[src], st3.at[src], s3_send.at[d - 1], s3_recv.at[d - 1], mate).wait_recv()
    top, tot, dot = merge(st3, NZ)
    put(st1, core, (top + jnp.log(tot), dot / tot))

    @pl.loop(0, LH)
    def _(h):
        cols = pl.ds(pl.multiple_of(h * HD, HD), HD)
        loc = pl.ds(RIM, TOK)
        prob = jnp.exp(srt[h] - st1[core, pl.ds(h, 1), :])
        ds = prob * (dpt[h] - st1[core, pl.ds(h + 4, 1), :])
        half = h // 2
        lane = pl.ds(pl.multiple_of((h % 2) * HD, HD), HD)
        rb[half, :, lane] = mm(prob.T.astype(BF), vc[loc, cols]).astype(BF)
        rb[2 + half, :, lane] = mm(ds.T.astype(BF), kc[loc, cols]).astype(BF)
        dkc[loc, cols] += mm(ds.astype(BF), glob(0, h))
        dvc[loc, cols] += mm(prob.astype(BF), glob(2, h))

    for t in (0, 1):
        sib_copy(t).start()

    def rs_copies(t):
        copies = []
        for d in range(1, NZ):
            to = (z + d) % NZ
            copies.append(remote(
                comb.at[t, pl.ds(pl.multiple_of(to * 32, 32), 32), :], rs.at[t, d - 1],
                rs_send.at[t, d - 1], rs_recv.at[t, d - 1], seq_of(y, to, core)))
        return copies

    def reduce_pair(t):
        sib_copy(t).wait()
        comb[t] = (rb[t * 2 + core].astype(F32) + sib[t].astype(F32)).astype(BF)
        for copy in rs_copies(t):
            copy.start()

    def og_copy(t):
        return remote(sl.at[t], ogat.at[t, s], og_send.at[t], og_recv.at[t], 0)

    def reduce_line(t):
        for copy in rs_copies(t):
            copy.wait()
        total = comb[t, pl.ds(pl.multiple_of(z * 32, 32), 32), :].astype(F32)
        for d in range(NZ - 1):
            total = total + rs[t, d].astype(F32)
        sl[t] = total.astype(BF)

        @pl.when(s > 0)
        def _():
            og_copy(t).start()

        @pl.when(owner)
        def _():
            ogat[t, 0] = total.astype(BF)

    def window_back(b):
        @pl.loop(0, LH)
        def _(h):
            rows, win, cols = spans(b, h)
            i = b * LH + h
            da = da_s[rows, cols]
            delta = jnp.sum(da.astype(F32) * attn_s[rows, cols].astype(F32), axis=1, keepdims=True)
            prob = ew[i] * cw[i]
            ds = prob * (dpw[i] - delta)
            dqa[rows, cols] += mm(ds.astype(BF), kc[win, cols])
            dkc[win, cols] += mm(ds.T.astype(BF), q_s[rows, cols])
            dvc[win, cols] += mm(prob.T.astype(BF), da)

    for t in (2, 3):
        reduce_pair(t)
    window_back(0)
    for t in (0, 1):
        reduce_pair(t)
    window_back(1)
    window_back(2)
    back = [
        remote(hbs.at[i], hbr.at[i], hb_send_sem.at[i], hb_recv_sem.at[i], prv) for i in range(2)
    ]
    hbs[0] = dkc[pl.ds(0, RIM), :].astype(BF)
    hbs[1] = dvc[pl.ds(0, RIM), :].astype(BF)

    @pl.when(s > 0)
    def _():
        for copy in back:
            copy.start()

    for t in (2, 3, 0, 1):
        reduce_line(t)
    window_back(3)

    @pl.when(s < NS - 1)
    def _():
        for i, acc in enumerate((dkc, dvc)):
            back[i].wait_recv()
            acc[pl.ds(RIM + BLK, RIM), :] += hbr[i].astype(F32)

    @pl.when(owner)
    def _():
        for t in (2, 3, 0, 1):
            whole = ogat.at[t, pl.ds(1, NS - 1)]
            pltpu.make_async_copy(whole, whole, og_recv.at[t]).wait()
            for zz in range(NZ):
                for cc in range(2):
                    total = ogat[t, zz * 2 + cc].astype(F32)
                    for yy in range(1, NY):
                        total = total + ogat[t, yy * 16 + zz * 2 + cc].astype(F32)
                    rt[t, zz * 32:(zz + 1) * 32, cc * 256:(cc + 1) * 256] = total.astype(BF)
            if t == 0:
                is_col = jnp.max(oh_s[...].astype(F32), axis=1, keepdims=True)
                attn_s[...] = jnp.where(
                    is_col > 0, mm(oh_s[...], rt[0]), attn_s[...].astype(F32)).astype(BF)
                for b in range(NB):
                    project(b)
            else:
                acc, rows = ((dqa, pl.ds(0, TOK)), (dkc, pl.ds(RIM, TOK)), (dvc, pl.ds(RIM, TOK)))[t - 1]
                acc[rows, :] += mm(oh_s[...], rt[t])

    gq_out[...] = (dqa[...] * SCALE).astype(BF)
    gk_out[...] = (dkc[pl.ds(RIM, TOK), :] * SCALE).astype(BF)
    gv_out[...] = dvc[pl.ds(RIM, TOK), :].astype(BF)

    for b in range(NB):
        rows = pl.ds(b * BLK, BLK)
        for copy in lx_copies(b):
            copy.wait()
        total = lp[x, rows, :].astype(F32)
        for d in range(NX - 1):
            total = total + lr[d, rows, :].astype(F32)
        lo_out[rows, :] = total.astype(BF)

    @pl.loop(0, NCH)
    def _(c):
        chunk_sends(c, lambda copy: copy.wait_send())

    for copy in st2_copies + st3_copies:
        copy.wait_send()

    @pl.when(s < NS - 1)
    def _():
        for copy in halo:
            copy.wait_send()

    @pl.when(s > 0)
    def _():
        for copy in back:
            copy.wait_send()
        for t in range(4):
            og_copy(t).wait_send()


def vmem(*shape, dtype=F32):
    return pltpu.VMEM(shape, dtype)


def on_device(queries, keys, values, out_weight, out_grad, global_pos, block_mask):
    dma = pltpu.SemaphoreType.DMA
    out = jax.ShapeDtypeStruct((TOK, COLS), BF)
    any_spec = pl.BlockSpec(memory_space=pl.ANY)
    vm_spec = pl.BlockSpec(memory_space=pltpu.VMEM)
    scratch = [
        vmem(TOK, COLS, dtype=BF), vmem(RIM + TOK, COLS, dtype=BF), vmem(RIM + TOK, COLS, dtype=BF),
        vmem(COLS, D, dtype=BF), vmem(TOK, D, dtype=BF), vmem(TOK, COLS, dtype=BF),
        vmem(TOK, GLB, dtype=BF), vmem(8, GLB, 256, dtype=BF), vmem(NB, BLK, WBLK * BLK),
        vmem(16, BLK, 512), vmem(16, BLK, 512), vmem(16, BLK, 1), vmem(16, BLK, 1), vmem(16, BLK, 1),
        vmem(TOK, COLS), vmem(16, BLK, GLB), vmem(TOK, COLS, dtype=BF),
        vmem(NX, TOK, COLS, dtype=BF), vmem(NX - 1, TOK, COLS, dtype=BF),
        vmem(RIM + TOK, COLS), vmem(RIM + TOK, COLS), vmem(TOK, COLS), vmem(GLB, COLS), vmem(GLB, COLS),
        vmem(2, RIM, COLS, dtype=BF), vmem(2, RIM, COLS, dtype=BF),
        vmem(2, 16, GLB), vmem(NY, 16, GLB), vmem(NZ, 16, GLB), vmem(LH, TOK, GLB), vmem(LH, TOK, GLB),
        vmem(8, GLB, 256, dtype=BF), vmem(4, GLB, 256, dtype=BF), vmem(4, GLB, 256, dtype=BF),
        vmem(4, NZ - 1, 32, 256, dtype=BF), vmem(4, 32, 256, dtype=BF), vmem(4, NS, 32, 256, dtype=BF),
        vmem(4, GLB, COLS, dtype=BF),
        dma((5,)), dma((NCH, 5)), dma((NCH,)), dma((2,)), dma((2,)), dma((2,)), dma((2,)),
        dma((NB, NX - 1)), dma((NB, NX - 1)), dma((1,)), dma((1,)), dma((NY - 1,)), dma((NY - 1,)),
        dma((NZ - 1,)), dma((NZ - 1,)), dma((4,)), dma((4,)), dma((4, NZ - 1)), dma((4, NZ - 1)),
        dma((4,)), dma((4,)),
    ]
    return pl.pallas_call(
        kernel,
        out_shape=(out,) * 4,
        in_specs=[any_spec] * 5 + [vm_spec, pl.BlockSpec(memory_space=pltpu.SMEM)],
        out_specs=(vm_spec,) * 4,
        scratch_shapes=scratch,
        compiler_params=pltpu.CompilerParams(vmem_limit_bytes=64000000, has_side_effects=True),
    )(queries, keys, values, out_weight, out_grad, global_pos.reshape(1, GLB), block_mask)


def solution(mesh):
    return jax.shard_map(
        on_device,
        mesh=mesh,
        in_specs=(
            P("seq", "head"), P("seq", "head"), P("seq", "head"),
            P("head", None), P("seq", None), P(), P("seq", None),
        ),
        out_specs=(P("seq", "head"),) * 4,
        check_vma=False,
    )
```

```python
import math

import jax
import jax.numpy as jnp
from jax import lax
from jax.experimental import pallas as pl
from jax.experimental.pallas import tpu as pltpu
from jax.sharding import PartitionSpec as P

HD = 128
BLK = 128
WBLK = 4
GLB = 256
TOK = 512
COLS = 512
LH = 4
NB = 4
RIM = 384
D = 2048
NY = 4
NZ = 8
NS = 64
NX = 4
NCH = 8
SCALE = 1.0 / math.sqrt(HD)
NEG = -1e30
F32 = jnp.float32
BF = jnp.bfloat16
MESH = pl.DeviceIdType.MESH


def mm(a, b):
    return lax.dot_general(a, b, (((1,), (0,)), ((), ())), preferred_element_type=F32)


def mm_t(a, b):
    return lax.dot_general(a, b, (((1,), (1,)), ((), ())), preferred_element_type=F32)


def flag(cond):
    return jnp.where(cond, 1, 0).astype(jnp.int32)


def kernel(
    q_hbm, k_hbm, v_hbm, w_hbm, og_hbm, gpos, bmask,
    lo_out, gq_out, gk_out, gv_out,
    q_s, kc, vc, w_s, og_s, da_s, oh_s, gbuf, bias,
    ew, dpw, mw, lw, cw, uw, pg_s, attn_s,
    lp, lr, dkc, dvc, dqa, dkg, dvg, hbs, hbr,
    st1, st2, st3, srt, dpt,
    rb, sib, comb, rs, sl, ogat, rt,
    ld_sem, bs_send, bs_recv, halo_send, halo_recv, hb_send_sem, hb_recv_sem,
    lx_send, lx_recv, s1_send, s1_recv, s2_send, s2_recv, s3_send, s3_recv,
    sib_send, sib_recv, rs_send, rs_recv, og_send, og_recv,
):
    s = lax.axis_index("seq")
    x = lax.axis_index("head")
    core = s % 2
    chip = s // 2
    z = chip % NZ
    y = chip // NZ
    owner = s == 0
    mate = s + 1 - 2 * core

    def seq_of(yy, zz, cc):
        return (yy * NZ + zz) * 2 + cc

    def remote(src, dst, ssem, rsem, to_seq):
        return pltpu.make_async_remote_copy(
            src_ref=src, dst_ref=dst, send_sem=ssem, recv_sem=rsem,
            device_id={"seq": to_seq}, device_id_type=MESH)

    loads = [
        pltpu.make_async_copy(k_hbm, kc.at[pl.ds(RIM, TOK)], ld_sem.at[0]),
        pltpu.make_async_copy(v_hbm, vc.at[pl.ds(RIM, TOK)], ld_sem.at[1]),
        pltpu.make_async_copy(q_hbm, q_s, ld_sem.at[2]),
        pltpu.make_async_copy(og_hbm, og_s, ld_sem.at[3]),
        pltpu.make_async_copy(w_hbm, w_s, ld_sem.at[4]),
    ]
    for copy in loads:
        copy.start()
    for copy in loads[:3]:
        copy.wait()

    nxt = jnp.minimum(s + 1, NS - 1)
    prv = jnp.maximum(s - 1, 0)
    halo = [
        remote(buf.at[pl.ds(RIM + BLK, RIM)], buf.at[pl.ds(0, RIM)], halo_send.at[i], halo_recv.at[i], nxt)
        for i, buf in enumerate((kc, vc))
    ]

    @pl.when(s < NS - 1)
    def _():
        for copy in halo:
            copy.start()

    @pl.when(owner)
    def _():
        kc[pl.ds(0, RIM), :] = jnp.zeros((RIM, COLS), BF)
        vc[pl.ds(0, RIM), :] = jnp.zeros((RIM, COLS), BF)

    hits = jnp.where(
        lax.broadcasted_iota(jnp.int32, (TOK, GLB), 0) == gpos[...], 1.0, 0.0).astype(F32)
    is_row = jnp.max(hits.T, axis=0, keepdims=True)
    own_f = jnp.where(owner, 1.0, 0.0).astype(F32)
    one_f = jnp.where(s == 1, 1.0, 0.0).astype(F32)
    oh_s[...] = (hits * own_f).astype(BF)

    def tree(a, na, b, nb):
        ap = flag(b == 0) * flag(a < na // 2)
        am = flag(b == 0) * (flag(a == 0) + flag(a > na // 2 + 1)) + flag(b != 0) * flag(a == 1)
        bp = flag(a != 0) * flag(b < nb // 2)
        bm = flag(a != 0) * (flag(b == 0) + flag(b > nb // 2 + 1))
        return ap, am, bp, bm

    zp0, zm0, yp0, ym0 = tree(z, NZ, y, NY)
    yp1, ym1, zp1, zm1 = tree(y, NY, z, NZ)
    dirs = (
        (zp0, zp1, seq_of(y, (z + 1) % NZ, core)),
        (zm0, zm1, seq_of(y, (z + NZ - 1) % NZ, core)),
        (yp0, yp1, seq_of((y + 1) % NY, z, core)),
        (ym0, ym1, seq_of((y + NY - 1) % NY, z, core)),
    )

    def chunk(c, half):
        start = pl.multiple_of((c % 2) * 128, 128)
        return gbuf.at[(c // 2) * 2 + half, pl.ds(start, 128), :]

    def chunk_copy(c, half, d, dev):
        return remote(chunk(c, half), chunk(c, half), bs_send.at[c, d], bs_recv.at[c, half], dev)

    def chunk_sends(c, act):
        for d, (c0, c1, dev) in enumerate(dirs):
            @pl.when(c0 * (1 - core) + c1 * core > 0)
            def _():
                act(chunk_copy(c, core, d, dev))

        @pl.when(owner)
        def _():
            act(chunk_copy(c, 1, 5, mate))

        @pl.when(s != 1)
        def _():
            act(chunk_copy(c, core, 4, mate))

    def gather(slot, src):
        got = mm(oh_s[...].astype(F32).T.astype(BF), src).astype(BF)
        gbuf[slot * 2, :, :] = got[:, :256]
        gbuf[slot * 2 + 1, :, :] = got[:, 256:]

    def send_chunks(first):
        @pl.loop(first, first + 4)
        def _(c):
            chunk_sends(c, lambda copy: copy.start())

    @pl.when(owner)
    def _():
        gather(0, q_s[...])
        gather(1, kc[pl.ds(RIM, TOK), :])
        send_chunks(0)

    for copy in loads[3:]:
        copy.wait()

    @pl.loop(0, NB)
    def _(b):
        rows = pl.ds(pl.multiple_of(b * BLK, BLK), BLK)
        da_s[rows, :] = mm_t(og_s[rows, :], w_s[...]).astype(BF)

    @pl.when(owner)
    def _():
        gather(2, da_s[...])
        gather(3, vc[pl.ds(RIM, TOK), :])
        send_chunks(4)
        is_col = jnp.max(oh_s[...].astype(F32), axis=1, keepdims=True)
        da_s[...] = jnp.where(is_col > 0, 0.0, da_s[...].astype(F32)).astype(BF)

    f_rim = is_row[:, 128:512] * one_f
    f_loc = is_row * own_f
    ii = lax.broadcasted_iota(jnp.int32, (BLK, BLK), 0)
    jj = lax.broadcasted_iota(jnp.int32, (BLK, BLK), 1)
    causal = jnp.where(jj <= ii, 0.0, NEG)
    for b in range(NB):
        for part in range(WBLK):
            r = WBLK - 1 - part
            ok = flag(bmask[b, r] == 1) * flag(s * NB + b - r >= 0)
            base = jnp.where(ok == 1, 0.0, NEG).astype(F32)
            at = b + part
            tok = f_rim[:, at * 128:(at + 1) * 128] if at < 3 else f_loc[:, (at - 3) * 128:(at - 2) * 128]
            tile = jnp.broadcast_to(tok * NEG + base, (BLK, BLK))
            if r == 0:
                tile = tile + causal
            bias[b, :, part * 128:(part + 1) * 128] = tile

    dkc[...] = jnp.zeros(dkc.shape, F32)
    dvc[...] = jnp.zeros(dvc.shape, F32)
    dkg[...] = jnp.zeros(dkg.shape, F32)
    dvg[...] = jnp.zeros(dvg.shape, F32)

    def spans(b, h):
        row0 = pl.multiple_of(b * BLK, BLK)
        return pl.ds(row0, BLK), pl.ds(row0, WBLK * BLK), pl.ds(pl.multiple_of(h * HD, HD), HD)

    def window_unit(u):
        b = NB - 1 - u // LH
        h = u % LH
        rows, win, cols = spans(b, h)
        sc = mm_t(q_s[rows, cols], kc[win, cols]) * SCALE + bias[b]
        top = jnp.max(sc, axis=1, keepdims=True)
        ex = jnp.exp(sc - top)
        i = b * LH + h
        ew[i] = ex
        mw[i] = top
        lw[i] = jnp.sum(ex, axis=1, keepdims=True)
        uw[rows, cols] = mm(ex.astype(BF), vc[win, cols])
        dpw[i] = mm_t(da_s[rows, cols], vc[win, cols])

    dz = jnp.minimum(z, NZ - z)
    dy = jnp.minimum(y, NY - y)
    turned = flag(core == 0) * flag(z == 0) * flag(y != 0) + flag(core == 1) * flag(y == 0) * flag(z != 0)
    depth = dz + dy + 2 * turned
    late_units = jnp.where(depth < 4, 4, 0)
    late_relay = jnp.where(depth < 4, 0, jnp.where(depth == 4, 4, jnp.where(depth == 5, 8, 16)))

    @pl.loop(0, 24)
    def _(t):
        u = jnp.where(t < 4, t, t - late_units)

        @pl.when((t >= 4) & (u == 4) & (s > 0))
        def _():
            for copy in halo:
                copy.wait_recv()

        @pl.when((t < 4) | ((u >= 4) & (u < 16)))
        def _():
            window_unit(u)

        c = t - late_relay

        @pl.when((c >= 0) & (c < NCH) & (s > 0))
        def _():
            chunk_copy(c, core, 0, mate).wait_recv()
            chunk_sends(c, lambda copy: copy.start())

    @pl.when(s > 0)
    def _():
        @pl.loop(0, NCH)
        def _(c):
            chunk_copy(c, 1 - core, 0, mate).wait_recv()

    def glob(slot, h):
        return gbuf[slot * 2 + h // 2, :, pl.ds(pl.multiple_of((h % 2) * HD, HD), HD)]

    @pl.loop(0, LH)
    def _(h):
        cols = pl.ds(pl.multiple_of(h * HD, HD), HD)
        loc = pl.ds(RIM, TOK)
        sc = mm_t(kc[loc, cols], glob(0, h)) * SCALE
        dp = mm_t(vc[loc, cols], glob(2, h))
        top = jnp.max(sc, axis=0, keepdims=True)
        ex = jnp.exp(sc - top)
        srt[h] = sc
        dpt[h] = dp
        st1[core, pl.ds(h, 1), :] = top
        st1[core, pl.ds(h + 4, 1), :] = jnp.sum(ex, axis=0, keepdims=True)
        st1[core, pl.ds(h + 8, 1), :] = jnp.sum(ex * dp, axis=0, keepdims=True)

    st1_copy = remote(st1.at[core], st1.at[core], s1_send.at[0], s1_recv.at[0], mate)
    st1_copy.start()

    def merge(ref, n):
        top = ref[0, 0:4, :]
        for i in range(1, n):
            top = jnp.maximum(top, ref[i, 0:4, :])
        tot = jnp.zeros((4, GLB), F32)
        dot = jnp.zeros((4, GLB), F32)
        for i in range(n):
            f = jnp.exp(ref[i, 0:4, :] - top)
            tot = tot + f * ref[i, 4:8, :]
            dot = dot + f * ref[i, 8:12, :]
        return top, tot, dot

    def put(ref, i, stats):
        for j, value in enumerate(stats):
            ref[i, j * 4:(j + 1) * 4, :] = value

    def lx_copies(b):
        rows = pl.ds(b * BLK, BLK)
        return [
            pltpu.make_async_remote_copy(
                src_ref=lp.at[(x + d) % NX, rows], dst_ref=lr.at[d - 1, rows],
                send_sem=lx_send.at[b, d - 1], recv_sem=lx_recv.at[b, d - 1],
                device_id={"head": (x + d) % NX}, device_id_type=MESH)
            for d in range(1, NX)
        ]

    def project(b):
        rows = pl.ds(b * BLK, BLK)
        for n in range(NX):
            lp[n, rows, :] = mm(attn_s[rows, :], w_s[:, n * COLS:(n + 1) * COLS]).astype(BF)
        for copy in lx_copies(b):
            copy.start()

    def forward(b):
        @pl.loop(0, LH)
        def _(h):
            rows, _, cols = spans(b, h)
            i = b * LH + h
            sg = mm_t(q_s[rows, cols], glob(1, h)) * SCALE
            top = jnp.maximum(mw[i], jnp.max(sg, axis=1, keepdims=True))
            eg = jnp.exp(sg - top)
            fac = jnp.exp(mw[i] - top)
            inv = 1.0 / (lw[i] * fac + jnp.sum(eg, axis=1, keepdims=True))
            out = (uw[rows, cols] * fac + mm(eg.astype(BF), glob(3, h))) * inv
            attn_s[rows, cols] = out.astype(BF)
            cw[i] = fac * inv
            pg_s[i] = eg * inv

        @pl.when(s > 0)
        def _():
            project(b)

    forward(0)
    st1_copy.wait()
    put(st2, y, merge(st1, 2))
    st2_copies = [
        remote(st2.at[y], st2.at[y], s2_send.at[d - 1], s2_recv.at[d - 1], seq_of((y + d) % NY, z, core))
        for d in range(1, NY)
    ]
    for copy in st2_copies:
        copy.start()
    forward(1)
    for d in range(1, NY):
        src = (y + NY - d) % NY
        remote(st2.at[src], st2.at[src], s2_send.at[d - 1], s2_recv.at[d - 1], mate).wait_recv()
    put(st3, z, merge(st2, NY))
    st3_copies = [
        remote(st3.at[z], st3.at[z], s3_send.at[d - 1], s3_recv.at[d - 1], seq_of(y, (z + d) % NZ, core))
        for d in range(1, NZ)
    ]
    for copy in st3_copies:
        copy.start()
    forward(2)
    forward(3)

    @pl.loop(0, NB * LH)
    def _(i):
        b = i // LH
        h = i % LH
        rows, _, cols = spans(b, h)
        da = da_s[rows, cols]
        delta = jnp.sum(da.astype(F32) * attn_s[rows, cols].astype(F32), axis=1, keepdims=True)
        pg = pg_s[i]
        ds = pg * (mm_t(da, glob(3, h)) - delta)
        dqa[rows, cols] = mm(ds.astype(BF), glob(1, h))
        dkg[:, cols] += mm(ds.astype(BF).T, q_s[rows, cols])
        dvg[:, cols] += mm(pg.astype(BF).T, da)

    def sib_copy(t):
        return remote(rb.at[t * 2 + 1 - core], sib.at[t], sib_send.at[t], sib_recv.at[t], mate)

    for t, part in ((2, dkg), (3, dvg)):
        for half in range(2):
            rb[t * 2 + half] = part[:, half * 256:(half + 1) * 256].astype(BF)
        sib_copy(t).start()

    for d in range(1, NZ):
        src = (z + NZ - d) % NZ
        remote(st3.at[src], st3.at[src], s3_send.at[d - 1], s3_recv.at[d - 1], mate).wait_recv()
    top, tot, dot = merge(st3, NZ)
    put(st1, core, (top + jnp.log(tot), dot / tot))

    @pl.loop(0, LH)
    def _(h):
        cols = pl.ds(pl.multiple_of(h * HD, HD), HD)
        loc = pl.ds(RIM, TOK)
        prob = jnp.exp(srt[h] - st1[core, pl.ds(h, 1), :])
        ds = prob * (dpt[h] - st1[core, pl.ds(h + 4, 1), :])
        half = h // 2
        lane = pl.ds(pl.multiple_of((h % 2) * HD, HD), HD)
        rb[half, :, lane] = mm(prob.astype(BF).T, vc[loc, cols]).astype(BF)
        rb[2 + half, :, lane] = mm(ds.astype(BF).T, kc[loc, cols]).astype(BF)
        dkc[loc, cols] += mm(ds.astype(BF), glob(0, h))
        dvc[loc, cols] += mm(prob.astype(BF), glob(2, h))

    for t in (0, 1):
        sib_copy(t).start()

    def rs_copies(t):
        copies = []
        for d in range(1, NZ):
            to = (z + d) % NZ
            copies.append(remote(
                comb.at[t, pl.ds(pl.multiple_of(to * 32, 32), 32), :], rs.at[t, d - 1],
                rs_send.at[t, d - 1], rs_recv.at[t, d - 1], seq_of(y, to, core)))
        return copies

    def reduce_pair(t):
        sib_copy(t).wait()
        comb[t] = (rb[t * 2 + core].astype(F32) + sib[t].astype(F32)).astype(BF)
        for copy in rs_copies(t):
            copy.start()

    def og_copy(t):
        return remote(sl.at[t], ogat.at[t, s], og_send.at[t], og_recv.at[t], 0)

    def reduce_line(t):
        for copy in rs_copies(t):
            copy.wait()
        total = comb[t, pl.ds(pl.multiple_of(z * 32, 32), 32), :].astype(F32)
        for d in range(NZ - 1):
            total = total + rs[t, d].astype(F32)
        sl[t] = total.astype(BF)

        @pl.when(s > 0)
        def _():
            og_copy(t).start()

        @pl.when(owner)
        def _():
            ogat[t, 0] = total.astype(BF)

    def window_back(b):
        @pl.loop(0, LH)
        def _(h):
            rows, win, cols = spans(b, h)
            i = b * LH + h
            da = da_s[rows, cols]
            delta = jnp.sum(da.astype(F32) * attn_s[rows, cols].astype(F32), axis=1, keepdims=True)
            prob = ew[i] * cw[i]
            ds = prob * (dpw[i] - delta)
            dqa[rows, cols] += mm(ds.astype(BF), kc[win, cols])
            dkc[win, cols] += mm(ds.astype(BF).T, q_s[rows, cols])
            dvc[win, cols] += mm(prob.astype(BF).T, da)

    for t in (2, 3):
        reduce_pair(t)
    window_back(0)
    for t in (0, 1):
        reduce_pair(t)
    window_back(1)
    window_back(2)
    back = [
        remote(hbs.at[i], hbr.at[i], hb_send_sem.at[i], hb_recv_sem.at[i], prv) for i in range(2)
    ]
    hbs[0] = dkc[pl.ds(0, RIM), :].astype(BF)
    hbs[1] = dvc[pl.ds(0, RIM), :].astype(BF)

    @pl.when(s > 0)
    def _():
        for copy in back:
            copy.start()

    for t in (2, 3, 0, 1):
        reduce_line(t)
    window_back(3)

    @pl.when(s < NS - 1)
    def _():
        for i, acc in enumerate((dkc, dvc)):
            back[i].wait_recv()
            acc[pl.ds(RIM + BLK, RIM), :] += hbr[i].astype(F32)

    @pl.when(owner)
    def _():
        for t in (2, 3, 0, 1):
            whole = ogat.at[t, pl.ds(1, NS - 1)]
            pltpu.make_async_copy(whole, whole, og_recv.at[t]).wait()
            for zz in range(NZ):
                for cc in range(2):
                    total = ogat[t, zz * 2 + cc].astype(F32)
                    for yy in range(1, NY):
                        total = total + ogat[t, yy * 16 + zz * 2 + cc].astype(F32)
                    rt[t, zz * 32:(zz + 1) * 32, cc * 256:(cc + 1) * 256] = total.astype(BF)
            if t == 0:
                is_col = jnp.max(oh_s[...].astype(F32), axis=1, keepdims=True)
                attn_s[...] = jnp.where(
                    is_col > 0, mm(oh_s[...], rt[0]), attn_s[...].astype(F32)).astype(BF)
                for b in range(NB):
                    project(b)
            else:
                acc, rows = ((dqa, pl.ds(0, TOK)), (dkc, pl.ds(RIM, TOK)), (dvc, pl.ds(RIM, TOK)))[t - 1]
                acc[rows, :] += mm(oh_s[...], rt[t])

    gq_out[...] = (dqa[...] * SCALE).astype(BF)
    gk_out[...] = (dkc[pl.ds(RIM, TOK), :] * SCALE).astype(BF)
    gv_out[...] = dvc[pl.ds(RIM, TOK), :].astype(BF)

    for b in range(NB):
        rows = pl.ds(b * BLK, BLK)
        for copy in lx_copies(b):
            copy.wait()
        total = lp[x, rows, :].astype(F32)
        for d in range(NX - 1):
            total = total + lr[d, rows, :].astype(F32)
        lo_out[rows, :] = total.astype(BF)

    @pl.loop(0, NCH)
    def _(c):
        chunk_sends(c, lambda copy: copy.wait_send())

    for copy in st2_copies + st3_copies:
        copy.wait_send()

    @pl.when(s < NS - 1)
    def _():
        for copy in halo:
            copy.wait_send()

    @pl.when(s > 0)
    def _():
        for copy in back:
            copy.wait_send()
        for t in range(4):
            og_copy(t).wait_send()


def hand_over(*refs):
    for src, dst in zip(refs[:4], refs[4:]):
        dst[...] = src[...]


def vmem(*shape, dtype=F32):
    return pltpu.VMEM(shape, dtype)


def on_device(queries, keys, values, out_weight, out_grad, global_pos, block_mask):
    dma = pltpu.SemaphoreType.DMA
    out = jax.ShapeDtypeStruct((TOK, COLS), BF)
    any_spec = pl.BlockSpec(memory_space=pl.ANY)
    vm_spec = pl.BlockSpec(memory_space=pltpu.VMEM)
    scratch = [
        vmem(TOK, COLS, dtype=BF), vmem(RIM + TOK, COLS, dtype=BF), vmem(RIM + TOK, COLS, dtype=BF),
        vmem(COLS, D, dtype=BF), vmem(TOK, D, dtype=BF), vmem(TOK, COLS, dtype=BF),
        vmem(TOK, GLB, dtype=BF), vmem(8, GLB, 256, dtype=BF), vmem(NB, BLK, WBLK * BLK),
        vmem(16, BLK, 512), vmem(16, BLK, 512), vmem(16, BLK, 1), vmem(16, BLK, 1), vmem(16, BLK, 1),
        vmem(TOK, COLS), vmem(16, BLK, GLB), vmem(TOK, COLS, dtype=BF),
        vmem(NX, TOK, COLS, dtype=BF), vmem(NX - 1, TOK, COLS, dtype=BF),
        vmem(RIM + TOK, COLS), vmem(RIM + TOK, COLS), vmem(TOK, COLS), vmem(GLB, COLS), vmem(GLB, COLS),
        vmem(2, RIM, COLS, dtype=BF), vmem(2, RIM, COLS, dtype=BF),
        vmem(2, 16, GLB), vmem(NY, 16, GLB), vmem(NZ, 16, GLB), vmem(LH, TOK, GLB), vmem(LH, TOK, GLB),
        vmem(8, GLB, 256, dtype=BF), vmem(4, GLB, 256, dtype=BF), vmem(4, GLB, 256, dtype=BF),
        vmem(4, NZ - 1, 32, 256, dtype=BF), vmem(4, 32, 256, dtype=BF), vmem(4, NS, 32, 256, dtype=BF),
        vmem(4, GLB, COLS, dtype=BF),
        dma((5,)), dma((NCH, 6)), dma((NCH, 2)), dma((2,)), dma((2,)), dma((2,)), dma((2,)),
        dma((NB, NX - 1)), dma((NB, NX - 1)), dma((1,)), dma((1,)), dma((NY - 1,)), dma((NY - 1,)),
        dma((NZ - 1,)), dma((NZ - 1,)), dma((4,)), dma((4,)), dma((4, NZ - 1)), dma((4, NZ - 1)),
        dma((4,)), dma((4,)),
    ]
    outs = pl.pallas_call(
        kernel,
        out_shape=(out,) * 4,
        in_specs=[any_spec] * 5 + [vm_spec, pl.BlockSpec(memory_space=pltpu.SMEM)],
        out_specs=(vm_spec,) * 4,
        scratch_shapes=scratch,
        compiler_params=pltpu.CompilerParams(vmem_limit_bytes=64000000, has_side_effects=True),
    )(queries, keys, values, out_weight, out_grad, global_pos.reshape(1, GLB), block_mask)
    tile = pl.BlockSpec((BLK, COLS), lambda i: (i, 0))
    return pl.pallas_call(
        hand_over,
        grid=(TOK // BLK,),
        out_shape=(out,) * 4,
        in_specs=[tile] * 4,
        out_specs=(tile,) * 4,
    )(*outs)


def solution(mesh):
    return jax.shard_map(
        on_device,
        mesh=mesh,
        in_specs=(
            P("seq", "head"), P("seq", "head"), P("seq", "head"),
            P("head", None), P("seq", None), P(), P("seq", None),
        ),
        out_specs=(P("seq", "head"),) * 4,
        check_vma=False,
    )
```

```python
import math

import jax
import jax.numpy as jnp
from jax import lax
from jax.experimental import pallas as pl
from jax.experimental.pallas import tpu as pltpu
from jax.sharding import PartitionSpec as P

HD = 128
BLK = 128
WBLK = 4
GLB = 256
TOK = 512
COLS = 512
LH = 4
NB = 4
RIM = 384
D = 2048
NY = 4
NZ = 8
NS = 64
NX = 4
NCH = 8
SCALE = 1.0 / math.sqrt(HD)
NEG = -1e30
F32 = jnp.float32
BF = jnp.bfloat16
MESH = pl.DeviceIdType.MESH


def mm(a, b):
    return lax.dot_general(a, b, (((1,), (0,)), ((), ())), preferred_element_type=F32)


def mm_t(a, b):
    return lax.dot_general(a, b, (((1,), (1,)), ((), ())), preferred_element_type=F32)


def flag(cond):
    return jnp.where(cond, 1, 0).astype(jnp.int32)


def kernel(
    q_hbm, k_hbm, v_hbm, w_hbm, og_hbm, gpos, bmask,
    lo_out, gq_out, gk_out, gv_out,
    q_s, kc, vc, w_s, og_s, da_s, oh_s, keep, gbuf, bias,
    ew, dpw, mw, lw, cw, uw, pg_s, attn_s,
    lp, lr, dkc, dvc, dqa, dkg, dvg, hbs, hbr,
    st1, st2, st3, srt, dpt,
    rb, sib, comb, rs, sl, own, yr, ol, rt, lpr, lrr,
    ld_sem, bs_send, bs_recv, halo_send, halo_recv, hb_send_sem, hb_recv_sem,
    lx_send, lx_recv, s1_send, s1_recv, s2_send, s2_recv, s3_send, s3_recv,
    sib_send, sib_recv, rs_send, rs_recv, yr_send, yr_recv, og_send, og_recv, lr_send, lr_recv,
):
    s = lax.axis_index("seq")
    x = lax.axis_index("head")
    core = s % 2
    chip = s // 2
    z = chip % NZ
    y = chip // NZ
    owner = s == 0
    mate = s + 1 - 2 * core

    def seq_of(yy, zz, cc):
        return (yy * NZ + zz) * 2 + cc

    def remote(src, dst, ssem, rsem, to_seq):
        return pltpu.make_async_remote_copy(
            src_ref=src, dst_ref=dst, send_sem=ssem, recv_sem=rsem,
            device_id={"seq": to_seq}, device_id_type=MESH)

    loads = [
        pltpu.make_async_copy(k_hbm, kc.at[pl.ds(RIM, TOK)], ld_sem.at[0]),
        pltpu.make_async_copy(v_hbm, vc.at[pl.ds(RIM, TOK)], ld_sem.at[1]),
        pltpu.make_async_copy(q_hbm, q_s, ld_sem.at[2]),
        pltpu.make_async_copy(og_hbm, og_s, ld_sem.at[3]),
        pltpu.make_async_copy(w_hbm, w_s, ld_sem.at[4]),
    ]
    for copy in loads:
        copy.start()
    for copy in loads[:3]:
        copy.wait()

    nxt = jnp.minimum(s + 1, NS - 1)
    prv = jnp.maximum(s - 1, 0)
    halo = [
        remote(buf.at[pl.ds(RIM + BLK, RIM)], buf.at[pl.ds(0, RIM)], halo_send.at[i], halo_recv.at[i], nxt)
        for i, buf in enumerate((kc, vc))
    ]

    @pl.when(s < NS - 1)
    def _():
        for copy in halo:
            copy.start()

    @pl.when(owner)
    def _():
        kc[pl.ds(0, RIM), :] = jnp.zeros((RIM, COLS), BF)
        vc[pl.ds(0, RIM), :] = jnp.zeros((RIM, COLS), BF)

    hits = jnp.where(
        lax.broadcasted_iota(jnp.int32, (TOK, GLB), 0) == gpos[...], 1.0, 0.0).astype(F32)
    is_row = jnp.max(hits.T, axis=0, keepdims=True)
    own_f = jnp.where(owner, 1.0, 0.0).astype(F32)
    one_f = jnp.where(s == 1, 1.0, 0.0).astype(F32)
    oh_s[...] = (hits * own_f).astype(BF)
    keep[...] = 1.0 - jnp.max(hits, axis=1, keepdims=True) * own_f

    def tree(a, na, b, nb):
        ap = flag(b == 0) * flag(a < na // 2)
        am = flag(b == 0) * (flag(a == 0) + flag(a > na // 2 + 1)) + flag(b != 0) * flag(a == 1)
        bp = flag(a != 0) * flag(b < nb // 2)
        bm = flag(a != 0) * (flag(b == 0) + flag(b > nb // 2 + 1))
        return ap, am, bp, bm

    zp0, zm0, yp0, ym0 = tree(z, NZ, y, NY)
    yp1, ym1, zp1, zm1 = tree(y, NY, z, NZ)
    dirs = (
        (zp0, zp1, seq_of(y, (z + 1) % NZ, core)),
        (zm0, zm1, seq_of(y, (z + NZ - 1) % NZ, core)),
        (yp0, yp1, seq_of((y + 1) % NY, z, core)),
        (ym0, ym1, seq_of((y + NY - 1) % NY, z, core)),
    )

    def chunk(c, half):
        start = pl.multiple_of((c % 2) * 128, 128)
        return gbuf.at[(c // 2) * 2 + half, pl.ds(start, 128), :]

    def chunk_copy(c, half, d, dev):
        return remote(chunk(c, half), chunk(c, half), bs_send.at[c, d], bs_recv.at[c, half], dev)

    def chunk_sends(c, act):
        for d, (c0, c1, dev) in enumerate(dirs):
            @pl.when(c0 * (1 - core) + c1 * core > 0)
            def _():
                act(chunk_copy(c, core, d, dev))

        @pl.when(owner)
        def _():
            act(chunk_copy(c, 1, 5, mate))

        @pl.when(s != 1)
        def _():
            act(chunk_copy(c, core, 4, mate))

    def gather(slot, src):
        got = mm(oh_s[...].astype(F32).T.astype(BF), src).astype(BF)
        gbuf[slot * 2, :, :] = got[:, :256]
        gbuf[slot * 2 + 1, :, :] = got[:, 256:]

    def send_chunks(first):
        @pl.loop(first, first + 4)
        def _(c):
            chunk_sends(c, lambda copy: copy.start())

    @pl.when(owner)
    def _():
        gather(0, q_s[...])
        gather(1, kc[pl.ds(RIM, TOK), :])
        send_chunks(0)

    for copy in loads[3:]:
        copy.wait()

    @pl.loop(0, NB)
    def _(b):
        rows = pl.ds(pl.multiple_of(b * BLK, BLK), BLK)
        da_s[rows, :] = mm_t(og_s[rows, :], w_s[...]).astype(BF)

    @pl.when(owner)
    def _():
        gather(2, da_s[...])
        gather(3, vc[pl.ds(RIM, TOK), :])
        send_chunks(4)
        da_s[...] = jnp.where(keep[...] > 0, da_s[...].astype(F32), 0.0).astype(BF)

    f_rim = is_row[:, 128:512] * one_f
    f_loc = is_row * own_f
    ii = lax.broadcasted_iota(jnp.int32, (BLK, BLK), 0)
    jj = lax.broadcasted_iota(jnp.int32, (BLK, BLK), 1)
    causal = jnp.where(jj <= ii, 0.0, NEG)
    for b in range(NB):
        for part in range(WBLK):
            r = WBLK - 1 - part
            ok = flag(bmask[b, r] == 1) * flag(s * NB + b - r >= 0)
            base = jnp.where(ok == 1, 0.0, NEG).astype(F32)
            at = b + part
            tok = f_rim[:, at * 128:(at + 1) * 128] if at < 3 else f_loc[:, (at - 3) * 128:(at - 2) * 128]
            tile = jnp.broadcast_to(tok * NEG + base, (BLK, BLK))
            if r == 0:
                tile = tile + causal
            bias[b, :, part * 128:(part + 1) * 128] = tile

    dkc[...] = jnp.zeros(dkc.shape, F32)
    dvc[...] = jnp.zeros(dvc.shape, F32)
    dkg[...] = jnp.zeros(dkg.shape, F32)
    dvg[...] = jnp.zeros(dvg.shape, F32)

    def spans(b, h):
        row0 = pl.multiple_of(b * BLK, BLK)
        return pl.ds(row0, BLK), pl.ds(row0, WBLK * BLK), pl.ds(pl.multiple_of(h * HD, HD), HD)

    def window_unit(u):
        b = NB - 1 - u // LH
        h = u % LH
        rows, win, cols = spans(b, h)
        sc = mm_t(q_s[rows, cols], kc[win, cols]) * SCALE + bias[b]
        top = jnp.max(sc, axis=1, keepdims=True)
        ex = jnp.exp(sc - top)
        i = b * LH + h
        ew[i] = ex
        mw[i] = top
        lw[i] = jnp.sum(ex, axis=1, keepdims=True)
        uw[rows, cols] = mm(ex.astype(BF), vc[win, cols])
        dpw[i] = mm_t(da_s[rows, cols], vc[win, cols])

    dz = jnp.minimum(z, NZ - z)
    dy = jnp.minimum(y, NY - y)
    turned = flag(core == 0) * flag(z == 0) * flag(y != 0) + flag(core == 1) * flag(y == 0) * flag(z != 0)
    depth = dz + dy + 2 * turned
    late_units = jnp.where(depth < 4, 4, 0)
    late_relay = jnp.where(depth < 4, 0, jnp.where(depth == 4, 4, jnp.where(depth == 5, 8, 16)))

    @pl.loop(0, 24)
    def _(t):
        u = jnp.where(t < 4, t, t - late_units)

        @pl.when((t >= 4) & (u == 4) & (s > 0))
        def _():
            for copy in halo:
                copy.wait_recv()

        @pl.when((t < 4) | ((u >= 4) & (u < 16)))
        def _():
            window_unit(u)

        c = t - late_relay

        @pl.when((c >= 0) & (c < NCH) & (s > 0))
        def _():
            chunk_copy(c, core, 0, mate).wait_recv()
            chunk_sends(c, lambda copy: copy.start())

    @pl.when(s > 0)
    def _():
        @pl.loop(0, NCH)
        def _(c):
            chunk_copy(c, 1 - core, 0, mate).wait_recv()

    def glob(slot, h):
        return gbuf[slot * 2 + h // 2, :, pl.ds(pl.multiple_of((h % 2) * HD, HD), HD)]

    @pl.loop(0, LH)
    def _(h):
        cols = pl.ds(pl.multiple_of(h * HD, HD), HD)
        loc = pl.ds(RIM, TOK)
        sc = mm_t(kc[loc, cols], glob(0, h)) * SCALE
        dp = mm_t(vc[loc, cols], glob(2, h))
        top = jnp.max(sc, axis=0, keepdims=True)
        ex = jnp.exp(sc - top)
        srt[h] = sc
        dpt[h] = dp
        st1[core, pl.ds(h, 1), :] = top
        st1[core, pl.ds(h + 4, 1), :] = jnp.sum(ex, axis=0, keepdims=True)
        st1[core, pl.ds(h + 8, 1), :] = jnp.sum(ex * dp, axis=0, keepdims=True)

    st1_copy = remote(st1.at[core], st1.at[core], s1_send.at[0], s1_recv.at[0], mate)
    st1_copy.start()

    def merge(ref, n):
        top = ref[0, 0:4, :]
        for i in range(1, n):
            top = jnp.maximum(top, ref[i, 0:4, :])
        tot = jnp.zeros((4, GLB), F32)
        dot = jnp.zeros((4, GLB), F32)
        for i in range(n):
            f = jnp.exp(ref[i, 0:4, :] - top)
            tot = tot + f * ref[i, 4:8, :]
            dot = dot + f * ref[i, 8:12, :]
        return top, tot, dot

    def put(ref, i, stats):
        for j, value in enumerate(stats):
            ref[i, j * 4:(j + 1) * 4, :] = value

    def lx_copies(b):
        rows = pl.ds(b * BLK, BLK)
        return [
            pltpu.make_async_remote_copy(
                src_ref=lp.at[(x + d) % NX, rows], dst_ref=lr.at[d - 1, rows],
                send_sem=lx_send.at[b, d - 1], recv_sem=lx_recv.at[b, d - 1],
                device_id={"head": (x + d) % NX}, device_id_type=MESH)
            for d in range(1, NX)
        ]

    def project(b):
        rows = pl.ds(b * BLK, BLK)
        for n in range(NX):
            lp[n, rows, :] = mm(attn_s[rows, :], w_s[:, n * COLS:(n + 1) * COLS]).astype(BF)
        for copy in lx_copies(b):
            copy.start()

    def forward(b):
        @pl.loop(0, LH)
        def _(h):
            rows, _, cols = spans(b, h)
            i = b * LH + h
            sg = mm_t(q_s[rows, cols], glob(1, h)) * SCALE
            top = jnp.maximum(mw[i], jnp.max(sg, axis=1, keepdims=True))
            eg = jnp.exp(sg - top)
            fac = jnp.exp(mw[i] - top)
            inv = 1.0 / (lw[i] * fac + jnp.sum(eg, axis=1, keepdims=True))
            out = (uw[rows, cols] * fac + mm(eg.astype(BF), glob(3, h))) * inv
            attn_s[rows, cols] = (out * keep[rows, :]).astype(BF)
            cw[i] = fac * inv
            pg_s[i] = eg * inv

        project(b)

    forward(0)
    st1_copy.wait()
    put(st2, y, merge(st1, 2))
    st2_copies = [
        remote(st2.at[y], st2.at[y], s2_send.at[d - 1], s2_recv.at[d - 1], seq_of((y + d) % NY, z, core))
        for d in range(1, NY)
    ]
    for copy in st2_copies:
        copy.start()
    forward(1)
    for d in range(1, NY):
        src = (y + NY - d) % NY
        remote(st2.at[src], st2.at[src], s2_send.at[d - 1], s2_recv.at[d - 1], mate).wait_recv()
    put(st3, z, merge(st2, NY))
    st3_copies = [
        remote(st3.at[z], st3.at[z], s3_send.at[d - 1], s3_recv.at[d - 1], seq_of(y, (z + d) % NZ, core))
        for d in range(1, NZ)
    ]
    for copy in st3_copies:
        copy.start()
    forward(2)
    forward(3)

    def glob_back(i):
        b = i // LH
        h = i % LH
        rows, _, cols = spans(b, h)
        da = da_s[rows, cols]
        delta = jnp.sum(da.astype(F32) * attn_s[rows, cols].astype(F32), axis=1, keepdims=True)
        pg = pg_s[i]
        ds = pg * (mm_t(da, glob(3, h)) - delta)
        dqa[rows, cols] = mm(ds.astype(BF), glob(1, h))
        dkg[:, cols] += mm(ds.astype(BF).T, q_s[rows, cols])
        dvg[:, cols] += mm(pg.astype(BF).T, da)

    def sib_copy(t):
        return remote(rb.at[t * 2 + 1 - core], sib.at[t], sib_send.at[t], sib_recv.at[t], mate)

    for d in range(1, NZ):
        src = (z + NZ - d) % NZ
        remote(st3.at[src], st3.at[src], s3_send.at[d - 1], s3_recv.at[d - 1], mate).wait_recv()
    top, tot, dot = merge(st3, NZ)
    put(st1, core, (top + jnp.log(tot), dot / tot))

    @pl.loop(0, LH)
    def _(h):
        cols = pl.ds(pl.multiple_of(h * HD, HD), HD)
        loc = pl.ds(RIM, TOK)
        prob = jnp.exp(srt[h] - st1[core, pl.ds(h, 1), :])
        ds = prob * (dpt[h] - st1[core, pl.ds(h + 4, 1), :])
        half = h // 2
        lane = pl.ds(pl.multiple_of((h % 2) * HD, HD), HD)
        rb[half, :, lane] = mm(prob.astype(BF).T, vc[loc, cols]).astype(BF)
        rb[2 + half, :, lane] = mm(ds.astype(BF).T, kc[loc, cols]).astype(BF)
        dkc[loc, cols] += mm(ds.astype(BF), glob(0, h))
        dvc[loc, cols] += mm(prob.astype(BF), glob(2, h))

    for t in (0, 1):
        sib_copy(t).start()

    def rs_copies(t):
        copies = []
        for d in range(1, NZ):
            to = (z + d) % NZ
            copies.append(remote(
                comb.at[t, pl.ds(pl.multiple_of(to * 32, 32), 32), :], rs.at[t, d - 1],
                rs_send.at[t, d - 1], rs_recv.at[t, d - 1], seq_of(y, to, core)))
        return copies

    def reduce_pair(t):
        sib_copy(t).wait()
        comb[t] = (rb[t * 2 + core].astype(F32) + sib[t].astype(F32)).astype(BF)
        for copy in rs_copies(t):
            copy.start()

    def yr_copy(t, d):
        return remote(sl.at[t], yr.at[t, d - 1], yr_send.at[t], yr_recv.at[t, d - 1], seq_of(0, z, core))

    def og_copy(t, i):
        place = rt.at[t, pl.ds(pl.multiple_of((i // 2) * 32, 32), 32), pl.ds(pl.multiple_of((i % 2) * 256, 256), 256)]
        return remote(ol.at[t], place, og_send.at[t], og_recv.at[t, i], 0)

    def reduce_line(t):
        for copy in rs_copies(t):
            copy.wait()
        total = comb[t, pl.ds(pl.multiple_of(z * 32, 32), 32), :].astype(F32)
        for d in range(NZ - 1):
            total = total + rs[t, d].astype(F32)

        @pl.when(y > 0)
        def _():
            sl[t] = total.astype(BF)
            yr_copy(t, y).start()

        @pl.when(y == 0)
        def _():
            own[t] = total

    def reduce_column(t):
        @pl.when(y == 0)
        def _():
            total = own[t]
            for d in range(1, NY):
                yr_copy(t, d).wait_recv()
                total = total + yr[t, d - 1].astype(F32)

            @pl.when(s > 0)
            def _():
                ol[t] = total.astype(BF)
                og_copy(t, s).start()

            @pl.when(owner)
            def _():
                rt[t, 0:32, 0:256] = total.astype(BF)

    def window_back(b):
        @pl.loop(0, LH)
        def _(h):
            rows, win, cols = spans(b, h)
            i = b * LH + h
            da = da_s[rows, cols]
            delta = jnp.sum(da.astype(F32) * attn_s[rows, cols].astype(F32), axis=1, keepdims=True)
            prob = ew[i] * cw[i]
            ds = prob * (dpw[i] - delta)
            dqa[rows, cols] += mm(ds.astype(BF), kc[win, cols])
            dkc[win, cols] += mm(ds.astype(BF).T, q_s[rows, cols])
            dvc[win, cols] += mm(prob.astype(BF).T, da)

    @pl.loop(0, 8)
    def _(i):
        glob_back(i)

    for t in (0, 1):
        reduce_pair(t)

    @pl.loop(8, 16)
    def _(i):
        glob_back(i)

    for t, part in ((2, dkg), (3, dvg)):
        for half in range(2):
            rb[t * 2 + half] = part[:, half * 256:(half + 1) * 256].astype(BF)
        sib_copy(t).start()
    window_back(0)
    window_back(1)
    for t in (0, 1):
        reduce_line(t)
    for t in (2, 3):
        reduce_pair(t)
    window_back(2)
    back = [
        remote(hbs.at[i], hbr.at[i], hb_send_sem.at[i], hb_recv_sem.at[i], prv) for i in range(2)
    ]
    hbs[0] = dkc[pl.ds(0, RIM), :].astype(BF)
    hbs[1] = dvc[pl.ds(0, RIM), :].astype(BF)

    @pl.when(s > 0)
    def _():
        for copy in back:
            copy.start()

    for t in (0, 1):
        reduce_column(t)
    window_back(3)
    for t in (2, 3):
        reduce_line(t)
    for t in (2, 3):
        reduce_column(t)

    def rows_here(t):
        for i in range(1, 2 * NZ):
            og_copy(t, i).wait_recv()

    def lo_rows(d):
        return pltpu.make_async_remote_copy(
            src_ref=lpr.at[(x + d) % NX], dst_ref=lrr.at[d - 1],
            send_sem=lr_send.at[d - 1], recv_sem=lr_recv.at[d - 1],
            device_id={"head": (x + d) % NX}, device_id_type=MESH)

    @pl.when(owner)
    def _():
        rows_here(0)
        for d in (2, 1, 3, 0):
            to = (x + d) % NX
            lpr[to] = mm(rt[0], w_s[:, pl.ds(pl.multiple_of(to * COLS, COLS), COLS)]).astype(BF)
            if d:
                lo_rows(d).start()
        for t, acc, rows in ((1, dqa, pl.ds(0, TOK)), (2, dkc, pl.ds(RIM, TOK)), (3, dvc, pl.ds(RIM, TOK))):
            rows_here(t)
            acc[rows, :] += mm(oh_s[...], rt[t])

    @pl.when(s < NS - 1)
    def _():
        for i, acc in enumerate((dkc, dvc)):
            back[i].wait_recv()
            acc[pl.ds(RIM + BLK, RIM), :] += hbr[i].astype(F32)

    gq_out[...] = (dqa[...] * SCALE).astype(BF)
    gk_out[...] = (dkc[pl.ds(RIM, TOK), :] * SCALE).astype(BF)
    gv_out[...] = dvc[pl.ds(RIM, TOK), :].astype(BF)

    for b in range(NB):
        rows = pl.ds(b * BLK, BLK)
        for copy in lx_copies(b):
            copy.wait()
        total = lp[x, rows, :].astype(F32)
        for d in range(NX - 1):
            total = total + lr[d, rows, :].astype(F32)
        lo_out[rows, :] = total.astype(BF)

    @pl.when(owner)
    def _():
        total = lpr[x].astype(F32)
        for d in range(1, NX):
            lo_rows(d).wait()
            total = total + lrr[d - 1].astype(F32)
        placed = mm(oh_s[...], total.astype(BF))
        lo_out[...] = (lo_out[...].astype(F32) + placed).astype(BF)

    @pl.loop(0, NCH)
    def _(c):
        chunk_sends(c, lambda copy: copy.wait_send())

    for copy in st2_copies + st3_copies:
        copy.wait_send()

    @pl.when(s < NS - 1)
    def _():
        for copy in halo:
            copy.wait_send()

    @pl.when(s > 0)
    def _():
        for copy in back:
            copy.wait_send()

    @pl.when(y > 0)
    def _():
        for t in range(4):
            yr_copy(t, y).wait_send()

    @pl.when((y == 0) & (s > 0))
    def _():
        for t in range(4):
            og_copy(t, s).wait_send()


def hand_over(*refs):
    for src, dst in zip(refs[:4], refs[4:]):
        dst[...] = src[...]


def vmem(*shape, dtype=F32):
    return pltpu.VMEM(shape, dtype)


def on_device(queries, keys, values, out_weight, out_grad, global_pos, block_mask):
    dma = pltpu.SemaphoreType.DMA
    out = jax.ShapeDtypeStruct((TOK, COLS), BF)
    any_spec = pl.BlockSpec(memory_space=pl.ANY)
    vm_spec = pl.BlockSpec(memory_space=pltpu.VMEM)
    scratch = [
        vmem(TOK, COLS, dtype=BF), vmem(RIM + TOK, COLS, dtype=BF), vmem(RIM + TOK, COLS, dtype=BF),
        vmem(COLS, D, dtype=BF), vmem(TOK, D, dtype=BF), vmem(TOK, COLS, dtype=BF),
        vmem(TOK, GLB, dtype=BF), vmem(TOK, 1), vmem(8, GLB, 256, dtype=BF), vmem(NB, BLK, WBLK * BLK),
        vmem(16, BLK, 512), vmem(16, BLK, 512), vmem(16, BLK, 1), vmem(16, BLK, 1), vmem(16, BLK, 1),
        vmem(TOK, COLS), vmem(16, BLK, GLB), vmem(TOK, COLS, dtype=BF),
        vmem(NX, TOK, COLS, dtype=BF), vmem(NX - 1, TOK, COLS, dtype=BF),
        vmem(RIM + TOK, COLS), vmem(RIM + TOK, COLS), vmem(TOK, COLS), vmem(GLB, COLS), vmem(GLB, COLS),
        vmem(2, RIM, COLS, dtype=BF), vmem(2, RIM, COLS, dtype=BF),
        vmem(2, 16, GLB), vmem(NY, 16, GLB), vmem(NZ, 16, GLB), vmem(LH, TOK, GLB), vmem(LH, TOK, GLB),
        vmem(8, GLB, 256, dtype=BF), vmem(4, GLB, 256, dtype=BF), vmem(4, GLB, 256, dtype=BF),
        vmem(4, NZ - 1, 32, 256, dtype=BF), vmem(4, 32, 256, dtype=BF), vmem(4, 32, 256),
        vmem(4, NY - 1, 32, 256, dtype=BF), vmem(4, 32, 256, dtype=BF),
        vmem(4, GLB, COLS, dtype=BF), vmem(NX, GLB, COLS, dtype=BF), vmem(NX - 1, GLB, COLS, dtype=BF),
        dma((5,)), dma((NCH, 6)), dma((NCH, 2)), dma((2,)), dma((2,)), dma((2,)), dma((2,)),
        dma((NB, NX - 1)), dma((NB, NX - 1)), dma((1,)), dma((1,)), dma((NY - 1,)), dma((NY - 1,)),
        dma((NZ - 1,)), dma((NZ - 1,)), dma((4,)), dma((4,)), dma((4, NZ - 1)), dma((4, NZ - 1)),
        dma((4,)), dma((4, NY - 1)), dma((4,)), dma((4, 2 * NZ)), dma((NX - 1,)), dma((NX - 1,)),
    ]
    outs = pl.pallas_call(
        kernel,
        out_shape=(out,) * 4,
        in_specs=[any_spec] * 5 + [vm_spec, pl.BlockSpec(memory_space=pltpu.SMEM)],
        out_specs=(vm_spec,) * 4,
        scratch_shapes=scratch,
        compiler_params=pltpu.CompilerParams(vmem_limit_bytes=64000000, has_side_effects=True),
    )(queries, keys, values, out_weight, out_grad, global_pos.reshape(1, GLB), block_mask)
    tile = pl.BlockSpec((BLK, COLS), lambda i: (i, 0))
    return pl.pallas_call(
        hand_over,
        grid=(TOK // BLK,),
        out_shape=(out,) * 4,
        in_specs=[tile] * 4,
        out_specs=(tile,) * 4,
    )(*outs)


def solution(mesh):
    return jax.shard_map(
        on_device,
        mesh=mesh,
        in_specs=(
            P("seq", "head"), P("seq", "head"), P("seq", "head"),
            P("head", None), P("seq", None), P(), P("seq", None),
        ),
        out_specs=(P("seq", "head"),) * 4,
        check_vma=False,
    )
```
